128 devices in a mesh: row: 16 (over y_hi, x, core), loop: 8 (over z, y_lo).
Axes of the slice: x: 4, y: 4 (y_hi: 2, y_lo: 2; y = y_hi * 2 + y_lo), z: 4, core: 2. Of those that a mesh axis runs over, the one named last changes fastest.
Arguments:
- features: bfloat16 [262144, 256], P(('row', 'loop')), may hold values from -6 to 6
- weight: bfloat16 [256, 256], replicated, may hold values from -0.375 to 0.375
- local_tiles: bfloat16 [16384, 128, 128], P(('row', 'loop')), may hold values from -0.1875 to 0.1875
- local_ids: int32 [16384], P(('row', 'loop')), may hold values from 0 to 255, as said below
- local_live: int32 [16384], P(('row', 'loop')), may hold values 0 or 1
- send_rows: int32 [128, 16, 256], P(('row', 'loop')), may hold values from 0 to 2047
- send_count: int32 [128, 16], P(('row', 'loop')), may hold values from 0 to 256, as said below
- edge_tiles: bfloat16 [36864, 128, 128], P(('row', 'loop')), may hold values from -0.1875 to 0.1875
- edge_ids: int32 [36864], P(('row', 'loop')), may hold values from 0 to 511, as said below
- edge_live: int32 [36864], P(('row', 'loop')), may hold values 0 or 1
- hub_feats: bfloat16 [2048, 256], P('loop'), may hold values from -6 to 6
- hub_adj: bfloat16 [262144, 2048], P(('row', 'loop')), may hold values from -0.1875 to 0.1875
- hub_live: int32 [2048, 16], P(('row', 'loop')), may hold values 0 or 1
Outputs:
- layer_out: bfloat16 [262144, 256], P(('row', 'loop'))
The draws below stay inside these ranges and needn't reach their ends.
Inputs may be any that keep to these rules, and one draw needn't show every extreme that they name: `local_ids`: each entry is i * 16 + j, a tile of one block's 16 x 16 grid; the 128 entries of one device are distinct. `edge_ids`: each entry is i * 32 + j, a tile of a 16 x 32 grid; the 288 entries of one device are distinct. Only the first send_count[d, s] slots of send_rows[d, s] are sent with data. For every loop index, all devices of that loop index send 256 rows to one common row index.
All inputs are finite; a program needn't handle non-finite values. No bound on the sum of `local_live` or of `edge_live` or of `hub_live` on one device may be relied on, other than what follows from the above.
Results may differ from the reference program's by a relative error of at most 0.005.
Values may be sent and summed in bfloat16 or wider, within the bound.
A program may use at most 256 MiB of HBM per device.

```python
import jax
import jax.numpy as jnp
from jax import lax

FEAT = 256
TILE = 128
ROWS_DEV = 2048
TILE_ROWS = 16
LOCAL_T = 128
SLOTS = 256
SLOT_TILES = 32
EDGE_T = 288
HUB = 2048
NODES = 262144
N_ROW = 16
N_LOOP = 8
DEVICES = 128


def draw_local_ids(key, part):
    key_list = jax.random.split(key, DEVICES)
    tile_grid = jax.vmap(lambda one_key: jax.random.permutation(one_key, TILE_ROWS * TILE_ROWS)[:LOCAL_T])(key_list)
    return tile_grid.reshape(DEVICES * LOCAL_T).astype(jnp.int32)


def draw_edge_ids(key, part):
    key_list = jax.random.split(jax.random.fold_in(key, 7), DEVICES)
    tile_grid = jax.vmap(lambda one_key: jax.random.permutation(one_key, TILE_ROWS * SLOT_TILES)[:EDGE_T])(key_list)
    return tile_grid.reshape(DEVICES * EDGE_T).astype(jnp.int32)


def draw_send_count(key, part):
    first_key = jax.random.fold_in(key, 11)
    second_key = jax.random.fold_in(key, 13)
    base_count = jax.random.randint(first_key, (DEVICES, N_ROW), 0, SLOTS + 1)
    hot_peer = jax.random.randint(second_key, (N_LOOP,), 0, N_ROW)
    loop_index = jnp.arange(DEVICES) % N_LOOP
    full_mask = hot_peer[loop_index][:, None] == jnp.arange(N_ROW)[None, :]
    return jnp.where(full_mask, SLOTS, base_count).astype(jnp.int32)


def set_ends(drawn, own_key, low, largest):
    shape = drawn.shape
    spot = [jax.random.randint(jax.random.fold_in(own_key, axis), (), 0, shape[axis]) for axis in range(len(shape))]
    drawn = drawn.at[tuple(spot)].set(low)
    longest = shape.index(max(shape))
    spot[longest] = (spot[longest] + 1) % shape[longest]
    return drawn.at[tuple(spot)].set(largest)


def steps_of(rng, extent, shards, least, top_value):
    loudness = 1.0
    for dim, blocks in shards:
        steps = jax.random.uniform(jax.random.fold_in(jax.random.fold_in(rng, 6), dim), (blocks,), jnp.float32, least / len(shards), top_value / len(shards))
        loudness = loudness * jnp.repeat(jnp.exp(steps), extent[dim] // blocks).reshape((-1,) + (1,) * (len(extent) - 1 - dim))
    return loudness


def normal_values(rng, extent, width, bound, cuts=(), kind=jnp.bfloat16):
    drawn = jax.random.normal(rng, extent, jnp.float32) * width
    if len(cuts) > 0:
        drawn = steps_of(rng, extent, cuts, -0.22, 0.18) * drawn
    return jnp.clip(drawn, min=-bound, max=bound).astype(kind)


def setup_inputs(seed: int = 0) -> dict:
    key_of = jax.random.split(jax.random.key(seed), 14)
    return {
        "features": normal_values(key_of[0], (NODES, FEAT), 1.0, 6.0, ((0, 128),)),
        "weight": normal_values(key_of[1], (FEAT, FEAT), FEAT ** -0.5, 0.375),
        "local_tiles": normal_values(key_of[2], (DEVICES * LOCAL_T, TILE, TILE), (ROWS_DEV // 2) ** -0.5, 0.1875, ((0, 128),)),
        "local_ids": draw_local_ids(jax.random.fold_in(key_of[13], 71), 0),
        "local_live": set_ends((jax.random.randint(key_of[4], (DEVICES * LOCAL_T,), 0, 4) < 3).astype(jnp.int32), jax.random.fold_in(key_of[4], 1), 0, 1),
        "send_rows": set_ends(jax.random.randint(key_of[5], (DEVICES, N_ROW, SLOTS), 0, ROWS_DEV), jax.random.fold_in(key_of[5], 1), 0, ROWS_DEV - 1).astype(jnp.int32),
        "send_count": draw_send_count(jax.random.fold_in(key_of[13], 71), 0),
        "edge_tiles": normal_values(key_of[7], (DEVICES * EDGE_T, TILE, TILE), (N_ROW * SLOTS // 4) ** -0.5, 0.1875, ((0, 128),)),
        "edge_ids": draw_edge_ids(jax.random.fold_in(key_of[13], 71), 0),
        "edge_live": set_ends((jax.random.randint(key_of[9], (DEVICES * EDGE_T,), 0, 4) < 3).astype(jnp.int32), jax.random.fold_in(key_of[9], 1), 0, 1),
        "hub_feats": normal_values(key_of[10], (HUB, FEAT), 1.0, 6.0, ((0, 8),)),
        "hub_adj": normal_values(key_of[11], (NODES, HUB), (HUB // 2) ** -0.5, 0.1875, ((0, 128),)),
        "hub_live": set_ends((jax.random.randint(key_of[12], (NODES // TILE, HUB // TILE), 0, 2) < 1).astype(jnp.int32), jax.random.fold_in(key_of[12], 1), 0, 1),
    }


def tile_term(tile_set, tile_ids, tile_live, panels, out_tiles, in_tiles):
    panel_grid = panels.reshape(in_tiles, TILE, FEAT)
    gathered = panel_grid[tile_ids % in_tiles]
    products = jnp.einsum("tab,tbf->taf", tile_set.astype(jnp.float32), gathered.astype(jnp.float32))
    row_select = (tile_ids // in_tiles)[:, None] == jnp.arange(out_tiles)[None, :]
    row_select = row_select.astype(jnp.float32) * tile_live[:, None].astype(jnp.float32)
    summed = jnp.einsum("tn,taf->naf", row_select, products, precision=lax.Precision.HIGHEST)
    return summed.reshape(out_tiles * TILE, FEAT)


def reference(features, weight, local_tiles, local_ids, local_live, send_rows, send_count, edge_tiles, edge_ids, edge_live, hub_feats, hub_adj, hub_live):
    devices = N_ROW * N_LOOP
    row_tiles = ROWS_DEV // TILE
    slot_cols = N_ROW * SLOTS // TILE
    blocks = features.reshape(devices, ROWS_DEV, FEAT)
    picked = jax.vmap(lambda block_rows, row_ids: block_rows[row_ids])(blocks, send_rows)
    kept_mask = jnp.arange(SLOTS)[None, None, :] < send_count[:, :, None]
    picked = jnp.where(kept_mask[..., None], picked, jnp.zeros((), jnp.bfloat16))
    received = picked.reshape(N_ROW, N_LOOP, N_ROW, SLOTS, FEAT).transpose(2, 1, 0, 3, 4).reshape(devices, N_ROW * SLOTS, FEAT)

    def one_block(inputs):
        block_feats, loc_set, loc_ids, loc_live, edg_set, edg_ids, edg_live, recv_rows, adj_rows, live_rows = inputs
        local_sum = tile_term(loc_set, loc_ids, loc_live, block_feats, row_tiles, row_tiles)
        edge_sum = tile_term(edg_set, edg_ids, edg_live, recv_rows, row_tiles, slot_cols)
        hub_mask = jnp.repeat(jnp.repeat(live_rows, TILE, 0), TILE, 1).astype(jnp.bfloat16)
        hub_sum = jnp.dot(adj_rows * hub_mask, hub_feats, preferred_element_type=jnp.float32)
        aggregated = (local_sum + edge_sum + hub_sum).astype(jnp.bfloat16)
        return jax.nn.relu(jnp.dot(aggregated, weight, preferred_element_type=jnp.float32)).astype(jnp.bfloat16)

    layer_out = lax.map(one_block, (
        blocks,
        local_tiles.reshape(devices, LOCAL_T, TILE, TILE),
        local_ids.reshape(devices, LOCAL_T),
        local_live.reshape(devices, LOCAL_T),
        edge_tiles.reshape(devices, EDGE_T, TILE, TILE),
        edge_ids.reshape(devices, EDGE_T),
        edge_live.reshape(devices, EDGE_T),
        received,
        hub_adj.reshape(devices, ROWS_DEV, HUB),
        hub_live.reshape(devices, row_tiles, HUB // TILE),
    ))
    return layer_out.reshape(devices * ROWS_DEV, FEAT)
```

```python
import functools

import jax
import jax.numpy as jnp
from jax import lax
from jax.experimental import pallas as pl
from jax.experimental.pallas import tpu as pltpu
from jax.sharding import PartitionSpec as P

MESH = pl.DeviceIdType.MESH
BF16 = jnp.bfloat16
F32 = jnp.float32
I32 = jnp.int32
TILE = 128
PIECE = 64
OWN = 12


def offset(k):
    return 1 - k // 8, (2 + 3 * ((k // 2) % 4)) % 4, k % 2


def partner(r, k, sign):
    dy, dx, dc = offset(k)
    y, x, c = r // 8, (r // 2) % 4, r % 2
    return ((y + dy) % 2) * 8 + ((x + sign * dx + 4) % 4) * 2 + (c + dc) % 2


def dot(a, b):
    return jnp.dot(a, b, preferred_element_type=F32)


def slot_table(edge_ids, edge_live, local_ids, local_live, hub_live):
    nedge, nloc, nrow = edge_ids.shape[0], local_ids.shape[0], hub_live.shape[0]
    ids = jnp.concatenate([edge_ids, local_ids + 512])
    live = jnp.concatenate([edge_live, local_live]) > 0
    slot = jnp.concatenate([jnp.arange(nedge) - nedge, jnp.arange(nloc) - nloc]).astype(I32)
    hit = jnp.logical_and(ids[:, None] == jnp.arange(768)[None, :], live[:, None])
    least = jnp.min(jnp.where(hit, slot[:, None], 0), axis=0)
    table = least + jnp.where(jnp.arange(768) < 512, nedge, nloc)
    hub = jnp.where(hub_live == 0, nrow, jnp.arange(nrow)[:, None])
    return jnp.concatenate([table, hub.reshape(-1)]).astype(I32)


def kernel(
    send_rows,
    tabs,
    send_count,
    features,
    weight,
    local_tiles,
    edge_tiles,
    hub_feats,
    hub_adj,
    out,
    feats,
    wts,
    loc,
    edg,
    hraw,
    hubf,
    a1,
    a2,
    send,
    recv,
    acc,
    outv,
    oh,
    rowsk,
    colk,
    in_sem,
    out_sem,
    ssem,
    rsem,
    hs_sem,
    hr_sem,
):
    r = lax.axis_index("row")
    l = lax.axis_index("loop")
    core = r % 2
    z, ylo = l // 2, l % 2
    sib = r + 1 - 2 * core
    nloc = local_tiles.shape[0]
    nedge = edge_tiles.shape[0]
    nrow = hub_adj.shape[0]

    def load(src, dst, n):
        return pltpu.make_async_copy(src, dst, in_sem.at[n])

    c_feat = load(features, feats, 0)
    c_feat.start()
    c_hub = load(hub_feats.at[pl.ds(core * TILE, TILE)], hubf.at[core, l], 1)
    c_hub.start()
    c_w = load(weight, wts, 2)
    c_w.start()
    c_loc = load(local_tiles, loc.at[pl.ds(0, nloc)], 3)
    c_loc.start()
    c_adj = load(hub_adj, hraw.at[pl.ds(0, nrow)], 4)
    c_adj.start()
    c_edge = load(edge_tiles, edg.at[pl.ds(0, nedge)], 5)
    c_edge.start()

    barrier = pltpu.get_barrier_semaphore()

    def greet(device):
        pl.semaphore_signal(barrier, inc=1, device_id=device, device_id_type=MESH)

    @pl.loop(0, 15)
    def _(n):
        greet({"row": (r + 1 + n) % 16, "loop": l})

    greet({"row": r, "loop": z * 2 + 1 - ylo})
    for dz in (1, 2, 3):
        greet({"row": r, "loop": ((z + dz) % 4) * 2 + ylo})

    rowsk[...] = jnp.full(rowsk.shape, -1, I32)
    slot = lax.broadcasted_iota(I32, (1, 4 * PIECE), 1)
    for k in range(16):
        s = partner(r, k, 1)
        row = send_rows[pl.ds(s, 1), :]
        rowsk[pl.ds(k, 1), :] = jnp.where(slot < send_count[0, s], row, -1)
    colk[...] = jnp.transpose(rowsk[...])

    loc[nloc] = jnp.zeros((TILE, TILE), BF16)
    edg[nedge] = jnp.zeros((TILE, TILE), BF16)
    hraw[nrow] = jnp.zeros((TILE, hraw.shape[2]), BF16)

    c_feat.wait()
    c_hub.wait()
    pl.semaphore_wait(barrier, 19)

    def remote(src, dst, s1, s2, device):
        return pltpu.make_async_remote_copy(
            src_ref=src, dst_ref=dst, send_sem=s1, recv_sem=s2, device_id=device, device_id_type=MESH
        )

    def piece(k, p, sign=1):
        return remote(
            send.at[k, pl.ds(p * PIECE, PIECE)],
            recv.at[p // 2, pl.ds(k * TILE + (p % 2) * PIECE, PIECE)],
            ssem.at[p, k],
            rsem.at[p, k],
            {"row": partner(r, k, 1), "loop": l},
        )

    def hub_step(n, lsrc, device):
        return remote(hubf.at[core, lsrc], hubf.at[core, lsrc], hs_sem.at[n], hr_sem.at[n], device)

    def hub_in(n, lsrc, half):
        return remote(
            hubf.at[half, lsrc], hubf.at[half, lsrc], hs_sem.at[n], hr_sem.at[n], {"row": sib, "loop": l}
        )

    l_y = z * 2 + 1 - ylo

    def zpeer(dz, own):
        return ((z + dz) % 4) * 2 + (ylo if own else 1 - ylo)

    hub_y = hub_step(0, l, {"row": r, "loop": l_y})
    hub_y.start()
    hub_z = [hub_step(dz, l, {"row": r, "loop": zpeer(dz, True)}) for dz in (1, 2, 3)]
    for c in hub_z:
        c.start()

    lane = lax.broadcasted_iota(I32, (4 * PIECE, TILE), 1)

    @pl.loop(0, 4)
    def _(p):
        cols = colk[pl.ds(pl.multiple_of(p * PIECE, PIECE), PIECE), :]
        for a in range(4):
            idx = jnp.concatenate(
                [jnp.broadcast_to(cols[:, k : k + 1], (PIECE, TILE)) for k in range(4 * a, 4 * a + 4)], 0
            )
            for c in range(feats.shape[0] // TILE):
                oh[:, c * TILE : (c + 1) * TILE] = jnp.where(idx == lane + c * TILE, 1.0, 0.0).astype(BF16)
            picked = dot(oh[...], feats[...]).astype(BF16)
            for d in range(4):
                k = 4 * a + d
                part = picked[d * PIECE : (d + 1) * PIECE]
                if k == OWN:
                    recv[p // 2, pl.ds(pl.multiple_of(k * TILE + (p % 2) * PIECE, PIECE), PIECE), :] = part
                else:
                    send[k, pl.ds(pl.multiple_of(p * PIECE, PIECE), PIECE), :] = part
                    piece(k, p).start()

    hub_in(0, l_y, core).wait_recv()
    hub_f = [hub_step(3 + dz, l_y, {"row": r, "loop": zpeer(dz, True)}) for dz in (1, 2, 3)]
    for c in hub_f:
        c.start()

    nm = 4
    mb = acc.shape[0] // nm

    def rows_of(m):
        return pl.ds(pl.multiple_of(m * mb, mb), mb)

    c_loc.wait()

    @pl.loop(0, 16)
    def _(i):
        at = pl.ds(pl.multiple_of(i * TILE, TILE), TILE)
        for j in range(16):
            a1[at, j * TILE : (j + 1) * TILE] = loc[tabs[512 + 16 * i + j]]

    @pl.loop(0, nm)
    def _(m):
        acc[rows_of(m), :] = dot(a1[rows_of(m), :], feats[...])

    for dz in (1, 2, 3):
        hub_in(dz, ((z + 4 - dz) % 4) * 2 + ylo, core).wait_recv()
        hub_in(3 + dz, ((z + 4 - dz) % 4) * 2 + 1 - ylo, core).wait_recv()
    hub_c = remote(hubf.at[core], hubf.at[core], hs_sem.at[7], hr_sem.at[7], {"row": sib, "loop": l})
    hub_c.start()

    c_adj.wait()

    @pl.loop(0, 16)
    def _(i):
        at = pl.ds(pl.multiple_of(i * TILE, TILE), TILE)
        for b in range(16):
            n = (b % 2) * 8 + b // 2
            a2[at, n * TILE : (n + 1) * TILE] = hraw[tabs[768 + 16 * i + b], :, b * TILE : (b + 1) * TILE]

    remote(hubf.at[1 - core], hubf.at[1 - core], hs_sem.at[7], hr_sem.at[7], {"row": sib, "loop": l}).wait_recv()

    @pl.loop(0, nm)
    def _(m):
        hub_all = hubf[...].reshape(16 * TILE, hubf.shape[3])
        acc[rows_of(m), :] += dot(a2[rows_of(m), :], hub_all)

    c_edge.wait()

    def lay_edges(h, a):
        @pl.loop(0, 16)
        def _(i):
            at = pl.ds(pl.multiple_of(i * TILE, TILE), TILE)
            for k in range(16):
                a[at, k * TILE : (k + 1) * TILE] = edg[tabs[32 * i + 2 * partner(r, k, -1) + h]]

    lay_edges(0, a1)
    lay_edges(1, a2)
    for p in (0, 1):
        for k in range(16):
            if k != OWN:
                piece(k, p).wait_recv()

    @pl.loop(0, nm)
    def _(m):
        acc[rows_of(m), :] += dot(a1[rows_of(m), :], recv[0])

    group = 4
    for g in range(4):
        span = slice(g * group * TILE, (g + 1) * group * TILE)
        for p in (2, 3):
            for k in range(g * group, (g + 1) * group):
                if k != OWN:
                    piece(k, p).wait_recv()
        if g < 3:

            @pl.loop(0, nm)
            def _(m):
                acc[rows_of(m), :] += dot(a2[rows_of(m), span], recv[1, span, :])

    c_w.wait()

    @pl.loop(0, nm)
    def _(m):
        at = rows_of(m)
        agg = (acc[at, :] + dot(a2[at, span], recv[1, span, :])).astype(BF16)
        outv[at, :] = jnp.maximum(dot(agg, wts[...]), 0.0).astype(BF16)
        pltpu.make_async_copy(outv.at[at], out.at[at], out_sem.at[m]).start()

    hub_y.wait_send()
    for c in hub_z + hub_f:
        c.wait_send()
    hub_c.wait_send()

    @pl.loop(0, 4)
    def _(p):
        for k in range(16):
            if k != OWN:
                piece(k, p).wait_send()

    @pl.loop(0, nm)
    def _(m):
        at = rows_of(m)
        pltpu.make_async_copy(outv.at[at], out.at[at], out_sem.at[m]).wait()


def per_device(
    features,
    weight,
    local_tiles,
    local_ids,
    local_live,
    send_rows,
    send_count,
    edge_tiles,
    edge_ids,
    edge_live,
    hub_feats,
    hub_adj,
    hub_live,
):
    rows, width = features.shape
    nloc, nedge = local_tiles.shape[0], edge_tiles.shape[0]
    tabs = slot_table(edge_ids, edge_live, local_ids, local_live, hub_live)
    vmem = pl.BlockSpec(memory_space=pltpu.VMEM)
    smem = pl.BlockSpec(memory_space=pltpu.SMEM)
    hbm = pl.BlockSpec(memory_space=pl.ANY)
    dma = pltpu.SemaphoreType.DMA
    return pl.pallas_call(
        kernel,
        out_shape=jax.ShapeDtypeStruct((rows, width), BF16),
        in_specs=[vmem, smem, smem, hbm, hbm, hbm, hbm, hbm, hbm],
        out_specs=hbm,
        scratch_shapes=[
            pltpu.VMEM((rows, width), BF16),
            pltpu.VMEM((width, width), BF16),
            pltpu.VMEM((nloc + 1, TILE, TILE), BF16),
            pltpu.VMEM((nedge + 1, TILE, TILE), BF16),
            pltpu.VMEM((rows // TILE + 1, TILE, 16 * TILE), BF16),
            pltpu.VMEM((2, 8, TILE, width), BF16),
            pltpu.VMEM((rows, 16 * TILE), BF16),
            pltpu.VMEM((rows, 16 * TILE), BF16),
            pltpu.VMEM((16, 4 * PIECE, width), BF16),
            pltpu.VMEM((2, 16 * TILE, width), BF16),
            pltpu.VMEM((rows, width), F32),
            pltpu.VMEM((rows, width), BF16),
            pltpu.VMEM((4 * PIECE, rows), BF16),
            pltpu.VMEM((TILE, 4 * PIECE), I32),
            pltpu.VMEM((4 * PIECE, TILE), I32),
            dma((6,)),
            dma((4,)),
            dma((4, 16)),
            dma((4, 16)),
            dma((8,)),
            dma((8,)),
        ],
        compiler_params=pltpu.CompilerParams(
            collective_id=0, has_side_effects=True, vmem_limit_bytes=58 * 1024 * 1024
        ),
        cost_estimate=pl.CostEstimate(flops=13 * 10**9, bytes_accessed=24 * 2**20, transcendentals=0),
    )(
        send_rows[0],
        tabs,
        send_count,
        features,
        weight,
        local_tiles,
        edge_tiles,
        hub_feats,
        hub_adj.reshape(rows // TILE, TILE, hub_adj.shape[1]),
    )


def solution(mesh):
    both = ("row", "loop")
    placed = (
        P(both, None),
        P(),
        P(both, None, None),
        P(both),
        P(both),
        P(both, None, None),
        P(both, None),
        P(both, None, None),
        P(both),
        P(both),
        P("loop", None),
        P(both, None),
        P(both, None),
    )
    return jax.shard_map(per_device, mesh=mesh, in_specs=placed, out_specs=P(both, None), check_vma=False)
```

```python
import functools

import jax
import jax.numpy as jnp
from jax import lax
from jax.experimental import pallas as pl
from jax.experimental.pallas import tpu as pltpu
from jax.sharding import PartitionSpec as P

MESH = pl.DeviceIdType.MESH
BF16 = jnp.bfloat16
F32 = jnp.float32
I32 = jnp.int32
I16 = jnp.int16
TILE = 128
PIECE = 64
OWN = 12


def offset(k):
    return 1 - k // 8, (2 + 3 * ((k // 2) % 4)) % 4, k % 2


def partner(r, k, sign):
    dy, dx, dc = offset(k)
    y, x, c = r // 8, (r // 2) % 4, r % 2
    return ((y + dy) % 2) * 8 + ((x + sign * dx + 4) % 4) * 2 + (c + dc) % 2


def dot(a, b):
    return jnp.dot(a, b, preferred_element_type=F32)


def slot_table(ids, live, bits, rows, cols, empty):
    slots = ids.shape[1]
    at_row = lax.broadcasted_iota(I32, (rows, slots), 0) == (ids >> bits)
    slot = lax.broadcasted_iota(I32, (rows, slots), 1) - empty
    value = jnp.where(jnp.logical_and(at_row, live > 0), slot, 0)
    col = ids & ((1 << bits) - 1)
    lane = lax.broadcasted_iota(I32, (rows, TILE), 1)
    table = jnp.zeros((rows, TILE), I32)
    for j in range(cols):
        least = jnp.min(jnp.where(col == j, value, 0), axis=1, keepdims=True)
        table = jnp.where(lane == j, least, table)
    return table + empty


def kernel(
    features,
    weight,
    local_tiles,
    local_ids,
    local_live,
    send_rows,
    send_count,
    edge_tiles,
    edge_ids,
    edge_live,
    hub_feats,
    hub_adj,
    hub_live,
    out,
    feats,
    wts,
    loc,
    edg,
    hraw,
    hubf,
    send,
    recv,
    acc,
    outv,
    rows_in,
    rowsk,
    colk,
    ids_e,
    live_e,
    ids_l,
    live_l,
    live_h,
    counts,
    tabv,
    tabs,
    in_sem,
    out_sem,
    ssem,
    rsem,
    hs_sem,
    hr_sem,
):
    r = lax.axis_index("row")
    l = lax.axis_index("loop")
    core = r % 2
    z, ylo = l // 2, l % 2
    sib = r + 1 - 2 * core
    nloc, nedge, nrow = local_tiles.shape[0], edge_tiles.shape[0], hub_adj.shape[0]

    def load(src, dst, n):
        return pltpu.make_async_copy(src, dst, in_sem.at[n])

    small = [
        load(src, dst, 6 + n)
        for n, (src, dst) in enumerate(
            [
                (send_rows, rows_in),
                (send_count, counts),
                (edge_ids, ids_e),
                (edge_live, live_e),
                (local_ids, ids_l),
                (local_live, live_l),
                (hub_live, live_h),
            ]
        )
    ]
    for c in small[:2]:
        c.start()
    def shard_half(half, owner):
        return pl.ds((half * 8 + owner) * TILE, TILE)

    c_feat = load(features, feats, 0)
    c_feat.start()
    c_hub = load(hub_feats.at[pl.ds(core * TILE, TILE)], hubf.at[shard_half(core, l)], 1)
    c_hub.start()
    for c in small[2:]:
        c.start()
    c_w = load(weight, wts, 2)
    c_w.start()
    c_loc = load(local_tiles, loc.at[pl.ds(0, nloc)], 3)
    c_loc.start()
    c_adj = load(hub_adj, hraw.at[pl.ds(0, nrow)], 4)
    c_adj.start()
    c_edge = load(edge_tiles, edg.at[pl.ds(0, nedge)], 5)
    c_edge.start()

    barrier = pltpu.get_barrier_semaphore()

    def greet(device):
        pl.semaphore_signal(barrier, inc=1, device_id=device, device_id_type=MESH)

    @pl.loop(0, 15)
    def _(n):
        greet({"row": (r + 1 + n) % 16, "loop": l})

    greet({"row": r, "loop": z * 2 + 1 - ylo})
    for dz in (1, 2, 3):
        greet({"row": r, "loop": ((z + dz) % 4) * 2 + ylo})

    for c in small[:2]:
        c.wait()
    rowsk[...] = jnp.full(rowsk.shape, -1, I32)
    slot = lax.broadcasted_iota(I32, (1, 4 * PIECE), 1)
    for k in range(16):
        s = partner(r, k, 1)
        row = rows_in[pl.ds(s, 1), :]
        rowsk[pl.ds(k, 1), :] = jnp.where(slot < counts[0, s], row, -1)
    colk[...] = jnp.transpose(rowsk[...])

    c_feat.wait()
    c_hub.wait()
    pl.semaphore_wait(barrier, 19)

    def remote(src, dst, s1, s2, device):
        return pltpu.make_async_remote_copy(
            src_ref=src, dst_ref=dst, send_sem=s1, recv_sem=s2, device_id=device, device_id_type=MESH
        )

    def piece(k, p, sign=1):
        return remote(
            send.at[k, pl.ds(p * PIECE, PIECE)],
            recv.at[p // 2, pl.ds(k * TILE + (p % 2) * PIECE, PIECE)],
            ssem.at[p, k],
            rsem.at[p, k],
            {"row": partner(r, k, 1), "loop": l},
        )

    def hub_step(n, lsrc, device):
        return remote(
            hubf.at[shard_half(core, lsrc)], hubf.at[shard_half(core, lsrc)], hs_sem.at[n], hr_sem.at[n], device
        )

    def hub_in(n, lsrc, half):
        at = hubf.at[shard_half(half, lsrc)]
        return remote(at, at, hs_sem.at[n], hr_sem.at[n], {"row": sib, "loop": l})

    l_y = z * 2 + 1 - ylo

    def zpeer(dz, own):
        return ((z + dz) % 4) * 2 + (ylo if own else 1 - ylo)

    hub_y = hub_step(0, l, {"row": r, "loop": l_y})
    hub_y.start()
    hub_z = [hub_step(dz, l, {"row": r, "loop": zpeer(dz, True)}) for dz in (1, 2, 3)]
    for c in hub_z:
        c.start()

    lane = lax.broadcasted_iota(I32, (4 * PIECE, TILE), 1).astype(I16)
    one, zero = jnp.ones(lane.shape, BF16), jnp.zeros(lane.shape, BF16)

    hub_f = [hub_step(3 + dz, l_y, {"row": r, "loop": zpeer(dz, True)}) for dz in (1, 2, 3)]

    def gather(p):
        cols = colk[pl.ds(pl.multiple_of(p * PIECE, PIECE), PIECE), :]
        for a in range(4):
            idx = jnp.concatenate(
                [jnp.broadcast_to(cols[:, k : k + 1], (PIECE, TILE)) for k in range(4 * a, 4 * a + 4)], 0
            )
            idx = idx.astype(I16)
            hot = [jnp.where(idx == lane + jnp.asarray(c * TILE, I16), one, zero) for c in range(feats.shape[0] // TILE)]
            picked = dot(jnp.concatenate(hot, 1), feats[...]).astype(BF16)
            for d in range(4):
                k = 4 * a + d
                part = picked[d * PIECE : (d + 1) * PIECE]
                if k == OWN:
                    recv[p // 2, pl.ds(pl.multiple_of(k * TILE + (p % 2) * PIECE, PIECE), PIECE), :] = part
                else:
                    send[k, pl.ds(pl.multiple_of(p * PIECE, PIECE), PIECE), :] = part
                    piece(k, p).start()

    @pl.loop(0, 2)
    def _(p):
        @pl.when(p == 1)
        def _():
            hub_in(0, l_y, core).wait_recv()
            for c in hub_f:
                c.start()

        gather(p)

    loc[nloc] = jnp.zeros((TILE, TILE), BF16)
    edg[nedge] = jnp.zeros((TILE, TILE), BF16)
    hraw[nrow] = jnp.zeros((TILE, hraw.shape[2]), BF16)
    for c in small[2:]:
        c.wait()
    tabv[0:16, :] = slot_table(ids_e[...][None, :], live_e[...][None, :], 5, 16, 32, nedge)
    tabv[16:32, :] = slot_table(ids_l[...], live_l[...], 4, 16, 16, nloc)
    cell_row = lax.broadcasted_iota(I32, live_h.shape, 0)
    tabv[32:48, 0:16] = jnp.where(live_h[...] == 0, nrow, cell_row)
    c_tab = load(tabv, tabs, 13)
    c_tab.start()

    def blocks(n):
        step = acc.shape[0] // n

        def over(body):
            @pl.loop(0, n)
            def _(m):
                body(m, pl.ds(pl.multiple_of(m * step, step), step))

        return over

    def laid(i0, n, cells):
        lines = [jnp.concatenate([cell(i0 + i) for cell in cells], 1) for i in range(n)]
        return jnp.concatenate(lines, 0)

    def local_cell(j):
        return lambda i: loc[tabs[16 + i, j]]

    def hub_cell(b):
        return lambda i: hraw[tabs[32 + i, b], :, b * TILE : (b + 1) * TILE]

    def edge_cell(k, h):
        col = 2 * partner(r, k, -1) + h
        return lambda i: edg[tabs[i, col]]

    c_tab.wait()
    c_loc.wait()
    cells = [local_cell(j) for j in range(16)]

    @blocks(4)
    def _(m, at):
        acc[at, :] = dot(laid(4 * m, 4, cells), feats[...])

    for dz in (1, 2, 3):
        hub_in(dz, ((z + 4 - dz) % 4) * 2 + ylo, core).wait_recv()
        hub_in(3 + dz, ((z + 4 - dz) % 4) * 2 + 1 - ylo, core).wait_recv()
    mine, other = pl.ds(core * 8 * TILE, 8 * TILE), pl.ds((1 - core) * 8 * TILE, 8 * TILE)
    hub_c = remote(hubf.at[mine], hubf.at[mine], hs_sem.at[7], hr_sem.at[7], {"row": sib, "loop": l})
    hub_c.start()

    @pl.loop(2, 4)
    def _(p):
        gather(p)

    c_edge.wait()
    for p in (0, 1):
        for k in range(16):
            if k != OWN:
                piece(k, p).wait_recv()
    cells = [edge_cell(k, 0) for k in range(16)]

    @blocks(4)
    def _(m, at):
        acc[at, :] += dot(laid(4 * m, 4, cells), recv[0])

    c_adj.wait()
    remote(hubf.at[other], hubf.at[other], hs_sem.at[7], hr_sem.at[7], {"row": sib, "loop": l}).wait_recv()
    cells = [hub_cell(b) for b in list(range(0, 16, 2)) + list(range(1, 16, 2))]

    @blocks(4)
    def _(m, at):
        acc[at, :] += dot(laid(4 * m, 4, cells), hubf[...])

    group = 4
    for g in range(4):
        span = slice(g * group * TILE, (g + 1) * group * TILE)
        for p in (2, 3):
            for k in range(g * group, (g + 1) * group):
                if k != OWN:
                    piece(k, p).wait_recv()
        cells = [edge_cell(k, 1) for k in range(g * group, (g + 1) * group)]
        if g < 3:

            @blocks(2)
            def _(m, at):
                acc[at, :] += dot(laid(8 * m, 8, cells), recv[1, span, :])

    c_w.wait()

    @blocks(4)
    def _(m, at):
        agg = (acc[at, :] + dot(laid(4 * m, 4, cells), recv[1, span, :])).astype(BF16)
        outv[at, :] = jnp.maximum(dot(agg, wts[...]), 0.0).astype(BF16)
        pltpu.make_async_copy(outv.at[at], out.at[at], out_sem.at[m]).start()

    hub_y.wait_send()
    for c in hub_z + hub_f:
        c.wait_send()
    hub_c.wait_send()

    @pl.loop(0, 4)
    def _(p):
        for k in range(16):
            if k != OWN:
                piece(k, p).wait_send()

    @blocks(4)
    def _(m, at):
        pltpu.make_async_copy(outv.at[at], out.at[at], out_sem.at[m]).wait()


def per_device(
    features,
    weight,
    local_tiles,
    local_ids,
    local_live,
    send_rows,
    send_count,
    edge_tiles,
    edge_ids,
    edge_live,
    hub_feats,
    hub_adj,
    hub_live,
):
    rows, width = features.shape
    nloc, nedge = local_tiles.shape[0], edge_tiles.shape[0]
    hbm = pl.BlockSpec(memory_space=pl.ANY)
    dma = pltpu.SemaphoreType.DMA
    return pl.pallas_call(
        kernel,
        out_shape=jax.ShapeDtypeStruct((rows, width), BF16),
        in_specs=[hbm] * 13,
        out_specs=hbm,
        scratch_shapes=[
            pltpu.VMEM((rows, width), BF16),
            pltpu.VMEM((width, width), BF16),
            pltpu.VMEM((nloc + 1, TILE, TILE), BF16),
            pltpu.VMEM((nedge + 1, TILE, TILE), BF16),
            pltpu.VMEM((rows // TILE + 1, TILE, 16 * TILE), BF16),
            pltpu.VMEM((16 * TILE, width), BF16),
            pltpu.VMEM((16, 4 * PIECE, width), BF16),
            pltpu.VMEM((2, 16 * TILE, width), BF16),
            pltpu.VMEM((rows, width), F32),
            pltpu.VMEM((rows, width), BF16),
            pltpu.VMEM((16, 4 * PIECE), I32),
            pltpu.VMEM((TILE, 4 * PIECE), I32),
            pltpu.VMEM((4 * PIECE, TILE), I32),
            pltpu.VMEM((nedge,), I32),
            pltpu.VMEM((nedge,), I32),
            pltpu.VMEM((1, nloc), I32),
            pltpu.VMEM((1, nloc), I32),
            pltpu.VMEM(hub_live.shape, I32),
            pltpu.SMEM(send_count.shape, I32),
            pltpu.VMEM((48, TILE), I32),
            pltpu.SMEM((48, TILE), I32),
            dma((14,)),
            dma((4,)),
            dma((4, 16)),
            dma((4, 16)),
            dma((8,)),
            dma((8,)),
        ],
        compiler_params=pltpu.CompilerParams(
            collective_id=0, has_side_effects=True, vmem_limit_bytes=60 * 1024 * 1024
        ),
        cost_estimate=pl.CostEstimate(flops=13 * 10**9, bytes_accessed=24 * 2**20, transcendentals=0),
    )(
        features,
        weight,
        local_tiles,
        local_ids[None, :],
        local_live[None, :],
        send_rows[0],
        send_count,
        edge_tiles,
        edge_ids,
        edge_live,
        hub_feats,
        hub_adj.reshape(rows // TILE, TILE, hub_adj.shape[1]),
        hub_live,
    )


def solution(mesh):
    both = ("row", "loop")
    placed = (
        P(both, None),
        P(),
        P(both, None, None),
        P(both),
        P(both),
        P(both, None, None),
        P(both, None),
        P(both, None, None),
        P(both),
        P(both),
        P("loop", None),
        P(both, None),
        P(both, None),
    )
    return jax.shard_map(per_device, mesh=mesh, in_specs=placed, out_specs=P(both, None), check_vma=False)
```

```python
import functools

import jax
import jax.numpy as jnp
from jax import lax
from jax.experimental import pallas as pl
from jax.experimental.pallas import tpu as pltpu
from jax.sharding import PartitionSpec as P

MESH = pl.DeviceIdType.MESH
BF16 = jnp.bfloat16
F32 = jnp.float32
I32 = jnp.int32
I16 = jnp.int16
TILE = 128
PIECE = 64
OWN = 6


def offset(k):
    dc, b, j = k // 8, (k // 4) % 2, k % 4
    return (1 + j + b) % 2, (2 + 3 * j) % 4, dc


def partner(r, k, sign):
    dy, dx, dc = offset(k)
    y, x, c = r // 8, (r // 2) % 4, r % 2
    return ((y + dy) % 2) * 8 + ((x + sign * dx + 4) % 4) * 2 + (c + dc) % 2


def dot(a, b):
    return jnp.dot(a, b, preferred_element_type=F32)


def slot_table(ids, live, bits, rows, cols, empty):
    slots = ids.shape[1]
    at_row = lax.broadcasted_iota(I32, (rows, slots), 0) == (ids >> bits)
    slot = lax.broadcasted_iota(I32, (rows, slots), 1) - empty
    value = jnp.where(jnp.logical_and(at_row, live > 0), slot, 0)
    col = ids & ((1 << bits) - 1)
    lane = lax.broadcasted_iota(I32, (rows, TILE), 1)
    table = jnp.zeros((rows, TILE), I32)
    for j in range(cols):
        least = jnp.min(jnp.where(col == j, value, 0), axis=1, keepdims=True)
        table = jnp.where(lane == j, least, table)
    return table + empty


def kernel(
    features,
    local_tiles,
    local_ids,
    local_live,
    send_rows,
    send_count,
    edge_tiles,
    edge_ids,
    edge_live,
    hub_feats,
    hub_adj,
    hub_live,
    out,
    feats,
    loc,
    edg,
    hraw,
    hubf,
    send,
    recv,
    acc,
    outv,
    rows_in,
    rowsk,
    colk,
    ids_e,
    live_e,
    ids_l,
    live_l,
    live_h,
    counts,
    tabv,
    tabs,
    in_sem,
    out_sem,
    ssem,
    rsem,
    hs_sem,
    hr_sem,
):
    r = lax.axis_index("row")
    l = lax.axis_index("loop")
    core = r % 2
    z, ylo = l // 2, l % 2
    sib = r + 1 - 2 * core
    nloc, nedge, nrow = local_tiles.shape[0], edge_tiles.shape[0], hub_adj.shape[0]

    def load(src, dst, n):
        return pltpu.make_async_copy(src, dst, in_sem.at[n])

    small = [
        load(src, dst, 6 + n)
        for n, (src, dst) in enumerate(
            [
                (send_rows, rows_in),
                (send_count, counts),
                (edge_ids, ids_e),
                (edge_live, live_e),
                (local_ids, ids_l),
                (local_live, live_l),
                (hub_live, live_h),
            ]
        )
    ]
    for c in small[:2]:
        c.start()
    def shard_half(half, owner):
        return pl.ds((half * 8 + owner) * TILE, TILE)

    c_feat = load(features, feats, 0)
    c_feat.start()
    c_hub = load(hub_feats.at[pl.ds(core * TILE, TILE)], hubf.at[shard_half(core, l)], 1)
    c_hub.start()
    for c in small[2:]:
        c.start()
    c_loc = load(local_tiles, loc.at[pl.ds(0, nloc)], 3)
    c_loc.start()
    c_adj = load(hub_adj, hraw.at[pl.ds(0, nrow)], 4)
    c_adj.start()
    c_edge = load(edge_tiles, edg.at[pl.ds(0, nedge)], 5)
    c_edge.start()

    barrier = pltpu.get_barrier_semaphore()

    def greet(device):
        pl.semaphore_signal(barrier, inc=1, device_id=device, device_id_type=MESH)

    @pl.loop(0, 15)
    def _(n):
        greet({"row": (r + 1 + n) % 16, "loop": l})

    greet({"row": r, "loop": z * 2 + 1 - ylo})
    for dz in (1, 2, 3):
        greet({"row": r, "loop": ((z + dz) % 4) * 2 + ylo})

    for c in small[:2]:
        c.wait()
    rowsk[...] = jnp.full(rowsk.shape, -1, I32)
    slot = lax.broadcasted_iota(I32, (1, 4 * PIECE), 1)
    for k in range(16):
        s = partner(r, k, 1)
        row = rows_in[pl.ds(s, 1), :]
        rowsk[pl.ds(k, 1), :] = jnp.where(slot < counts[0, s], row, -1)
    colk[...] = jnp.transpose(rowsk[...])

    c_feat.wait()
    c_hub.wait()
    pl.semaphore_wait(barrier, 19)

    def remote(src, dst, s1, s2, device):
        return pltpu.make_async_remote_copy(
            src_ref=src, dst_ref=dst, send_sem=s1, recv_sem=s2, device_id=device, device_id_type=MESH
        )

    def piece(k, p, sign=1):
        return remote(
            send.at[k, pl.ds(p * PIECE, PIECE)],
            recv.at[p // 2, pl.ds(k * TILE + (p % 2) * PIECE, PIECE)],
            ssem.at[p, k],
            rsem.at[p, k],
            {"row": partner(r, k, 1), "loop": l},
        )

    def hub_step(n, lsrc, device):
        return remote(
            hubf.at[shard_half(core, lsrc)], hubf.at[shard_half(core, lsrc)], hs_sem.at[n], hr_sem.at[n], device
        )

    def hub_in(n, lsrc, half):
        at = hubf.at[shard_half(half, lsrc)]
        return remote(at, at, hs_sem.at[n], hr_sem.at[n], {"row": sib, "loop": l})

    l_y = z * 2 + 1 - ylo

    def zpeer(dz, own):
        return ((z + dz) % 4) * 2 + (ylo if own else 1 - ylo)

    hub_y = hub_step(0, l, {"row": r, "loop": l_y})
    hub_y.start()
    hub_z = [hub_step(dz, l, {"row": r, "loop": zpeer(dz, True)}) for dz in (1, 2, 3)]
    for c in hub_z:
        c.start()

    lane = lax.broadcasted_iota(I32, (4 * PIECE, TILE), 1).astype(I16)
    one, zero = jnp.ones(lane.shape, BF16), jnp.zeros(lane.shape, BF16)

    hub_f = [hub_step(3 + dz, l_y, {"row": r, "loop": zpeer(dz, True)}) for dz in (1, 2, 3)]

    def gather(p, a):
        cols = colk[pl.ds(pl.multiple_of(p * PIECE, PIECE), PIECE), :]
        idx = jnp.concatenate(
            [jnp.broadcast_to(cols[:, k : k + 1], (PIECE, TILE)) for k in range(4 * a, 4 * a + 4)], 0
        )
        idx = idx.astype(I16)
        hot = [jnp.where(idx == lane + jnp.asarray(c * TILE, I16), one, zero) for c in range(feats.shape[0] // TILE)]
        picked = dot(jnp.concatenate(hot, 1), feats[...]).astype(BF16)
        for d in range(4):
            k = 4 * a + d
            part = picked[d * PIECE : (d + 1) * PIECE]
            if k == OWN:
                recv[p // 2, pl.ds(pl.multiple_of(k * TILE + (p % 2) * PIECE, PIECE), PIECE), :] = part
            else:
                send[k, pl.ds(pl.multiple_of(p * PIECE, PIECE), PIECE), :] = part
                piece(k, p).start()

    @pl.loop(0, 2)
    def _(p):
        @pl.when(p == 1)
        def _():
            hub_in(0, l_y, core).wait_recv()
            for c in hub_f:
                c.start()

        for a in range(4):
            gather(p, a)

    loc[nloc] = jnp.zeros((TILE, TILE), BF16)
    edg[nedge] = jnp.zeros((TILE, TILE), BF16)
    hraw[nrow] = jnp.zeros((TILE, hraw.shape[2]), BF16)
    for c in small[2:]:
        c.wait()
    tabv[0:16, :] = slot_table(ids_e[...][None, :], live_e[...][None, :], 5, 16, 32, nedge)
    tabv[16:32, :] = slot_table(ids_l[...], live_l[...], 4, 16, 16, nloc)
    cell_row = lax.broadcasted_iota(I32, live_h.shape, 0)
    tabv[32:48, 0:16] = jnp.where(live_h[...] == 0, nrow, cell_row)
    c_tab = load(tabv, tabs, 13)
    c_tab.start()

    def blocks(n):
        step = acc.shape[0] // n

        def over(body):
            @pl.loop(0, n)
            def _(m):
                body(m, pl.ds(pl.multiple_of(m * step, step), step))

        return over

    def laid(i0, n, cells):
        lines = [jnp.concatenate([cell(i0 + i) for cell in cells], 1) for i in range(n)]
        return jnp.concatenate(lines, 0)

    def local_cell(j):
        return lambda i: loc[tabs[16 + i, j]]

    def hub_cell(b):
        return lambda i: hraw[tabs[32 + i, b], :, b * TILE : (b + 1) * TILE]

    def edge_cell(k, h):
        col = 2 * partner(r, k, -1) + h
        return lambda i: edg[tabs[i, col]]

    c_tab.wait()
    c_loc.wait()
    cells = [local_cell(j) for j in range(16)]

    @blocks(4)
    def _(m, at):
        acc[at, :] = dot(laid(4 * m, 4, cells), feats[...])

    for dz in (1, 2, 3):
        hub_in(dz, ((z + 4 - dz) % 4) * 2 + ylo, core).wait_recv()
        hub_in(3 + dz, ((z + 4 - dz) % 4) * 2 + 1 - ylo, core).wait_recv()
    mine, other = pl.ds(core * 8 * TILE, 8 * TILE), pl.ds((1 - core) * 8 * TILE, 8 * TILE)
    hub_c = remote(hubf.at[mine], hubf.at[mine], hs_sem.at[7], hr_sem.at[7], {"row": sib, "loop": l})
    hub_c.start()

    for a in range(4):

        @pl.loop(2, 4)
        def _(p):
            gather(p, a)

    c_edge.wait()
    for p in (0, 1):
        for k in range(16):
            if k != OWN:
                piece(k, p).wait_recv()
    cells = [edge_cell(k, 0) for k in range(16)]

    @blocks(4)
    def _(m, at):
        acc[at, :] += dot(laid(4 * m, 4, cells), recv[0])

    c_adj.wait()
    remote(hubf.at[other], hubf.at[other], hs_sem.at[7], hr_sem.at[7], {"row": sib, "loop": l}).wait_recv()
    cells = [hub_cell(b) for b in list(range(0, 16, 2)) + list(range(1, 16, 2))]

    @blocks(4)
    def _(m, at):
        acc[at, :] += dot(laid(4 * m, 4, cells), hubf[...])

    def edge_group(first, last):
        for k in range(first, last):
            if k != OWN:
                for p in (2, 3):
                    piece(k, p).wait_recv()
        return slice(first * TILE, last * TILE), [edge_cell(k, 1) for k in range(first, last)]

    span, cells = edge_group(0, 8)

    @blocks(4)
    def _(m, at):
        acc[at, :] += dot(laid(4 * m, 4, cells), recv[1, span, :])

    span2, cells2 = edge_group(8, 12)

    @blocks(2)
    def _(m, at):
        acc[at, :] += dot(laid(8 * m, 8, cells2), recv[1, span2, :])

    span3, cells3 = edge_group(12, 16)

    @blocks(4)
    def _(m, at):
        outv[at, :] = (acc[at, :] + dot(laid(4 * m, 4, cells3), recv[1, span3, :])).astype(BF16)
        pltpu.make_async_copy(outv.at[at], out.at[at], out_sem.at[m]).start()

    hub_y.wait_send()
    for c in hub_z + hub_f:
        c.wait_send()
    hub_c.wait_send()

    @pl.loop(0, 4)
    def _(p):
        for k in range(16):
            if k != OWN:
                piece(k, p).wait_send()

    @blocks(4)
    def _(m, at):
        pltpu.make_async_copy(outv.at[at], out.at[at], out_sem.at[m]).wait()


def per_device(
    features,
    weight,
    local_tiles,
    local_ids,
    local_live,
    send_rows,
    send_count,
    edge_tiles,
    edge_ids,
    edge_live,
    hub_feats,
    hub_adj,
    hub_live,
):
    rows, width = features.shape
    nloc, nedge = local_tiles.shape[0], edge_tiles.shape[0]
    hbm = pl.BlockSpec(memory_space=pl.ANY)
    dma = pltpu.SemaphoreType.DMA
    agg = pl.pallas_call(
        kernel,
        out_shape=jax.ShapeDtypeStruct((rows, width), BF16),
        in_specs=[hbm] * 12,
        out_specs=hbm,
        scratch_shapes=[
            pltpu.VMEM((rows, width), BF16),
            pltpu.VMEM((nloc + 1, TILE, TILE), BF16),
            pltpu.VMEM((nedge + 1, TILE, TILE), BF16),
            pltpu.VMEM((rows // TILE + 1, TILE, 16 * TILE), BF16),
            pltpu.VMEM((16 * TILE, width), BF16),
            pltpu.VMEM((16, 4 * PIECE, width), BF16),
            pltpu.VMEM((2, 16 * TILE, width), BF16),
            pltpu.VMEM((rows, width), F32),
            pltpu.VMEM((rows, width), BF16),
            pltpu.VMEM((16, 4 * PIECE), I32),
            pltpu.VMEM((TILE, 4 * PIECE), I32),
            pltpu.VMEM((4 * PIECE, TILE), I32),
            pltpu.VMEM((nedge,), I32),
            pltpu.VMEM((nedge,), I32),
            pltpu.VMEM((1, nloc), I32),
            pltpu.VMEM((1, nloc), I32),
            pltpu.VMEM(hub_live.shape, I32),
            pltpu.SMEM(send_count.shape, I32),
            pltpu.VMEM((48, TILE), I32),
            pltpu.SMEM((48, TILE), I32),
            dma((14,)),
            dma((4,)),
            dma((4, 16)),
            dma((4, 16)),
            dma((8,)),
            dma((8,)),
        ],
        compiler_params=pltpu.CompilerParams(
            collective_id=0, has_side_effects=True, vmem_limit_bytes=60 * 1024 * 1024
        ),
        cost_estimate=pl.CostEstimate(flops=13 * 10**9, bytes_accessed=24 * 2**20, transcendentals=0),
    )(
        features,
        local_tiles,
        local_ids[None, :],
        local_live[None, :],
        send_rows[0],
        send_count,
        edge_tiles,
        edge_ids,
        edge_live,
        hub_feats,
        hub_adj.reshape(rows // TILE, TILE, hub_adj.shape[1]),
        hub_live,
    )
    return jnp.maximum(dot(agg, weight), 0.0).astype(BF16)


def solution(mesh):
    both = ("row", "loop")
    placed = (
        P(both, None),
        P(),
        P(both, None, None),
        P(both),
        P(both),
        P(both, None, None),
        P(both, None),
        P(both, None, None),
        P(both),
        P(both),
        P("loop", None),
        P(both, None),
        P(both, None),
    )
    return jax.shard_map(per_device, mesh=mesh, in_specs=placed, out_specs=P(both, None), check_vma=False)
```

```python
import functools

import jax
import jax.numpy as jnp
from jax import lax
from jax.experimental import pallas as pl
from jax.experimental.pallas import tpu as pltpu
from jax.sharding import PartitionSpec as P

MESH = pl.DeviceIdType.MESH
BF16 = jnp.bfloat16
F32 = jnp.float32
I32 = jnp.int32
I16 = jnp.int16
TILE = 128
PIECE = 64
OWN = 6


def offset(k):
    dc, b, j = k // 8, (k // 4) % 2, k % 4
    return (1 + j + b) % 2, (2 + 3 * j) % 4, dc


def partner(r, k, sign):
    dy, dx, dc = offset(k)
    y, x, c = r // 8, (r // 2) % 4, r % 2
    return ((y + dy) % 2) * 8 + ((x + sign * dx + 4) % 4) * 2 + (c + dc) % 2


def dot(a, b):
    return jnp.dot(a, b, preferred_element_type=F32)


def slot_table(ids, live, bits, rows, cols, empty):
    slots = ids.shape[1]
    at_row = lax.broadcasted_iota(I32, (rows, slots), 0) == (ids >> bits)
    slot = lax.broadcasted_iota(I32, (rows, slots), 1) - empty
    value = jnp.where(jnp.logical_and(at_row, live > 0), slot, 0)
    col = ids & ((1 << bits) - 1)
    lane = lax.broadcasted_iota(I32, (rows, TILE), 1)
    table = jnp.zeros((rows, TILE), I32)
    for j in range(cols):
        least = jnp.min(jnp.where(col == j, value, 0), axis=1, keepdims=True)
        table = jnp.where(lane == j, least, table)
    return table + empty


def kernel(
    features,
    local_tiles,
    local_ids,
    local_live,
    send_rows,
    send_count,
    edge_tiles,
    edge_ids,
    edge_live,
    hub_feats,
    hub_adj,
    hub_live,
    out,
    feats,
    loc,
    edg,
    hraw,
    hubf,
    send,
    recv,
    acc,
    rows_in,
    rowsk,
    colk,
    ids_e,
    live_e,
    ids_l,
    live_l,
    live_h,
    counts,
    tabv,
    tabs,
    in_sem,
    ssem,
    rsem,
    hs_sem,
    hr_sem,
):
    r = lax.axis_index("row")
    l = lax.axis_index("loop")
    core = r % 2
    z, ylo = l // 2, l % 2
    sib = r + 1 - 2 * core
    nloc, nedge, nrow = local_tiles.shape[0], edge_tiles.shape[0], hub_adj.shape[0]

    def load(src, dst, n):
        return pltpu.make_async_copy(src, dst, in_sem.at[n])

    small = [
        load(src, dst, 6 + n)
        for n, (src, dst) in enumerate(
            [
                (send_rows, rows_in),
                (send_count, counts),
                (edge_ids, ids_e),
                (edge_live, live_e),
                (local_ids, ids_l),
                (local_live, live_l),
                (hub_live, live_h),
            ]
        )
    ]
    for c in small[:2]:
        c.start()
    def shard_half(half, owner):
        return pl.ds((half * 8 + owner) * TILE, TILE)

    c_feat = load(features, feats, 0)
    c_feat.start()
    c_hub = load(hub_feats.at[pl.ds(core * TILE, TILE)], hubf.at[shard_half(core, l)], 1)
    c_hub.start()
    for c in small[2:]:
        c.start()
    c_loc = load(local_tiles, loc.at[pl.ds(0, nloc)], 3)
    c_loc.start()
    c_adj = load(hub_adj, hraw.at[pl.ds(0, nrow)], 4)
    c_adj.start()
    c_edge = load(edge_tiles, edg.at[pl.ds(0, nedge)], 5)
    c_edge.start()

    barrier = pltpu.get_barrier_semaphore()

    def greet(device):
        pl.semaphore_signal(barrier, inc=1, device_id=device, device_id_type=MESH)

    @pl.loop(0, 15)
    def _(n):
        greet({"row": (r + 1 + n) % 16, "loop": l})

    greet({"row": r, "loop": z * 2 + 1 - ylo})
    for dz in (1, 2, 3):
        greet({"row": r, "loop": ((z + dz) % 4) * 2 + ylo})

    for c in small[:2]:
        c.wait()
    rowsk[...] = jnp.full(rowsk.shape, -1, I32)
    slot = lax.broadcasted_iota(I32, (1, 4 * PIECE), 1)
    for k in range(16):
        s = partner(r, k, 1)
        row = rows_in[pl.ds(s, 1), :]
        rowsk[pl.ds(k, 1), :] = jnp.where(slot < counts[0, s], row, -1)
    colk[...] = jnp.transpose(rowsk[...])

    c_feat.wait()
    c_hub.wait()
    pl.semaphore_wait(barrier, 19)

    def remote(src, dst, s1, s2, device):
        return pltpu.make_async_remote_copy(
            src_ref=src, dst_ref=dst, send_sem=s1, recv_sem=s2, device_id=device, device_id_type=MESH
        )

    def piece(k, p, sign=1):
        return remote(
            send.at[k, pl.ds(p * PIECE, PIECE)],
            recv.at[p // 2, pl.ds(k * TILE + (p % 2) * PIECE, PIECE)],
            ssem.at[p, k],
            rsem.at[p, k],
            {"row": partner(r, k, 1), "loop": l},
        )

    def hub_step(n, lsrc, device):
        return remote(
            hubf.at[shard_half(core, lsrc)], hubf.at[shard_half(core, lsrc)], hs_sem.at[n], hr_sem.at[n], device
        )

    def hub_in(n, lsrc, half):
        at = hubf.at[shard_half(half, lsrc)]
        return remote(at, at, hs_sem.at[n], hr_sem.at[n], {"row": sib, "loop": l})

    l_y = z * 2 + 1 - ylo

    def zpeer(dz, own):
        return ((z + dz) % 4) * 2 + (ylo if own else 1 - ylo)

    hub_y = hub_step(0, l, {"row": r, "loop": l_y})
    hub_y.start()
    hub_z = [hub_step(dz, l, {"row": r, "loop": zpeer(dz, True)}) for dz in (1, 2, 3)]
    for c in hub_z:
        c.start()

    lane = lax.broadcasted_iota(I32, (4 * PIECE, TILE), 1).astype(I16)
    one, zero = jnp.ones(lane.shape, BF16), jnp.zeros(lane.shape, BF16)

    hub_f = [hub_step(3 + dz, l_y, {"row": r, "loop": zpeer(dz, True)}) for dz in (1, 2, 3)]

    def gather(p, a):
        cols = colk[pl.ds(pl.multiple_of(p * PIECE, PIECE), PIECE), :]
        idx = jnp.concatenate(
            [jnp.broadcast_to(cols[:, k : k + 1], (PIECE, TILE)) for k in range(4 * a, 4 * a + 4)], 0
        )
        idx = idx.astype(I16)
        hot = [jnp.where(idx == lane + jnp.asarray(c * TILE, I16), one, zero) for c in range(feats.shape[0] // TILE)]
        picked = dot(jnp.concatenate(hot, 1), feats[...]).astype(BF16)
        for d in range(4):
            k = 4 * a + d
            part = picked[d * PIECE : (d + 1) * PIECE]
            if k == OWN:
                recv[p // 2, pl.ds(pl.multiple_of(k * TILE + (p % 2) * PIECE, PIECE), PIECE), :] = part
            else:
                send[k, pl.ds(pl.multiple_of(p * PIECE, PIECE), PIECE), :] = part
                piece(k, p).start()

    @pl.loop(0, 2)
    def _(p):
        @pl.when(p == 1)
        def _():
            hub_in(0, l_y, core).wait_recv()
            for c in hub_f:
                c.start()

        for a in range(4):
            gather(p, a)

    loc[nloc] = jnp.zeros((TILE, TILE), BF16)
    edg[nedge] = jnp.zeros((TILE, TILE), BF16)
    hraw[nrow] = jnp.zeros((TILE, hraw.shape[2]), BF16)
    for c in small[2:]:
        c.wait()
    tabv[0:16, :] = slot_table(ids_e[...][None, :], live_e[...][None, :], 5, 16, 32, nedge)
    tabv[16:32, :] = slot_table(ids_l[...], live_l[...], 4, 16, 16, nloc)
    cell_row = lax.broadcasted_iota(I32, live_h.shape, 0)
    tabv[32:48, 0:16] = jnp.where(live_h[...] == 0, nrow, cell_row)
    c_tab = load(tabv, tabs, 13)
    c_tab.start()

    def blocks(n):
        step = acc.shape[0] // n

        def over(body):
            @pl.loop(0, n)
            def _(m):
                body(m, pl.ds(pl.multiple_of(m * step, step), step))

        return over

    def laid(i0, n, cells):
        lines = [jnp.concatenate([cell(i0 + i) for cell in cells], 1) for i in range(n)]
        return jnp.concatenate(lines, 0)

    def local_cell(j):
        return lambda i: loc[tabs[16 + i, j]]

    def hub_cell(b):
        return lambda i: hraw[tabs[32 + i, b], :, b * TILE : (b + 1) * TILE]

    def edge_cell(k, h):
        col = 2 * partner(r, k, -1) + h
        return lambda i: edg[tabs[i, col]]

    c_tab.wait()
    c_loc.wait()
    cells = [local_cell(j) for j in range(16)]

    @blocks(4)
    def _(m, at):
        acc[at, :] = dot(laid(4 * m, 4, cells), feats[...])

    for dz in (1, 2, 3):
        hub_in(dz, ((z + 4 - dz) % 4) * 2 + ylo, core).wait_recv()
        hub_in(3 + dz, ((z + 4 - dz) % 4) * 2 + 1 - ylo, core).wait_recv()
    mine, other = pl.ds(core * 8 * TILE, 8 * TILE), pl.ds((1 - core) * 8 * TILE, 8 * TILE)
    hub_c = remote(hubf.at[mine], hubf.at[mine], hs_sem.at[7], hr_sem.at[7], {"row": sib, "loop": l})
    hub_c.start()

    for a in range(4):

        @pl.loop(2, 4)
        def _(p):
            gather(p, a)

    c_edge.wait()
    for p in (0, 1):
        for k in range(16):
            if k != OWN:
                piece(k, p).wait_recv()
    cells = [edge_cell(k, 0) for k in range(16)]

    @blocks(4)
    def _(m, at):
        acc[at, :] += dot(laid(4 * m, 4, cells), recv[0])

    c_adj.wait()
    remote(hubf.at[other], hubf.at[other], hs_sem.at[7], hr_sem.at[7], {"row": sib, "loop": l}).wait_recv()
    cells = [hub_cell(b) for b in list(range(0, 16, 2)) + list(range(1, 16, 2))]

    @blocks(4)
    def _(m, at):
        acc[at, :] += dot(laid(4 * m, 4, cells), hubf[...])

    def edge_group(first, last):
        for k in range(first, last):
            if k != OWN:
                for p in (2, 3):
                    piece(k, p).wait_recv()
        return slice(first * TILE, last * TILE), [edge_cell(k, 1) for k in range(first, last)]

    span, cells = edge_group(0, 8)

    @blocks(4)
    def _(m, at):
        acc[at, :] += dot(laid(4 * m, 4, cells), recv[1, span, :])

    span2, cells2 = edge_group(8, 12)

    @blocks(2)
    def _(m, at):
        acc[at, :] += dot(laid(8 * m, 8, cells2), recv[1, span2, :])

    span3, cells3 = edge_group(12, 16)

    @blocks(4)
    def _(m, at):
        out[at, :] = (acc[at, :] + dot(laid(4 * m, 4, cells3), recv[1, span3, :])).astype(BF16)


    hub_y.wait_send()
    for c in hub_z + hub_f:
        c.wait_send()
    hub_c.wait_send()

    @pl.loop(0, 4)
    def _(p):
        for k in range(16):
            if k != OWN:
                piece(k, p).wait_send()


def per_device(
    features,
    weight,
    local_tiles,
    local_ids,
    local_live,
    send_rows,
    send_count,
    edge_tiles,
    edge_ids,
    edge_live,
    hub_feats,
    hub_adj,
    hub_live,
):
    rows, width = features.shape
    nloc, nedge = local_tiles.shape[0], edge_tiles.shape[0]
    hbm = pl.BlockSpec(memory_space=pltpu.HBM)
    dma = pltpu.SemaphoreType.DMA
    agg = pl.pallas_call(
        kernel,
        out_shape=jax.ShapeDtypeStruct((rows, width), BF16),
        in_specs=[hbm] * 12,
        out_specs=pl.BlockSpec(memory_space=pltpu.VMEM),
        scratch_shapes=[
            pltpu.VMEM((rows, width), BF16),
            pltpu.VMEM((nloc + 1, TILE, TILE), BF16),
            pltpu.VMEM((nedge + 1, TILE, TILE), BF16),
            pltpu.VMEM((rows // TILE + 1, TILE, 16 * TILE), BF16),
            pltpu.VMEM((16 * TILE, width), BF16),
            pltpu.VMEM((16, 4 * PIECE, width), BF16),
            pltpu.VMEM((2, 16 * TILE, width), BF16),
            pltpu.VMEM((rows, width), F32),
            pltpu.VMEM((16, 4 * PIECE), I32),
            pltpu.VMEM((TILE, 4 * PIECE), I32),
            pltpu.VMEM((4 * PIECE, TILE), I32),
            pltpu.VMEM((nedge,), I32),
            pltpu.VMEM((nedge,), I32),
            pltpu.VMEM((1, nloc), I32),
            pltpu.VMEM((1, nloc), I32),
            pltpu.VMEM(hub_live.shape, I32),
            pltpu.SMEM(send_count.shape, I32),
            pltpu.VMEM((48, TILE), I32),
            pltpu.SMEM((48, TILE), I32),
            dma((14,)),
            dma((4, 16)),
            dma((4, 16)),
            dma((8,)),
            dma((8,)),
        ],
        compiler_params=pltpu.CompilerParams(
            collective_id=0, has_side_effects=True, vmem_limit_bytes=40 * 1024 * 1024
        ),
        cost_estimate=pl.CostEstimate(flops=13 * 10**9, bytes_accessed=24 * 2**20, transcendentals=0),
    )(*[pltpu.with_memory_space_constraint(v, pltpu.HBM) for v in (
        features,
        local_tiles,
        local_ids[None, :],
        local_live[None, :],
        send_rows[0],
        send_count,
        edge_tiles,
        edge_ids,
        edge_live,
        hub_feats,
        hub_adj.reshape(rows // TILE, TILE, hub_adj.shape[1]),
        hub_live,
    )])
    return jnp.maximum(dot(agg, weight), 0.0).astype(BF16)


def solution(mesh):
    both = ("row", "loop")
    placed = (
        P(both, None),
        P(),
        P(both, None, None),
        P(both),
        P(both),
        P(both, None, None),
        P(both, None),
        P(both, None, None),
        P(both),
        P(both),
        P("loop", None),
        P(both, None),
        P(both, None),
    )
    return jax.shard_map(per_device, mesh=mesh, in_specs=placed, out_specs=P(both, None), check_vma=False)
```
